32 devices in a mesh: tm: 4 (over y, core), strip: 8 (over z, x).
Axes of the slice: x: 2, y: 2, z: 4, core: 2. Of those that a mesh axis runs over, the one named last changes fastest.
Arguments:
- start_state: float32 [16, 64, 128], P(None, 'strip'), may hold values from -20 to 20
- trajectory: float32 [8, 16, 64, 128], P('tm', None, 'strip'), may hold values from -20 to 20
- history: float32 [3, 8, 16, 64, 128], P(None, 'tm', None, 'strip'), may hold values from -6 to 6
- history_length: int32 [8], P('tm'), may hold values from 1 to 3
- timesteps: int32 [8], P('tm'), may hold values from 0 to 999
- step_size: float32 [8], P('tm'), may hold values from 0.05 to 0.2
- mix_table: int32 [8, 8], replicated, may hold values from -64 to 128, as said below
- time_table: float32 [1000, 320], replicated, may hold values from -6 to 6
- conv_in: bfloat16 [9, 320, 16], replicated, may hold values from -0.5 to 0.5
- norm_gain: float32 [320], replicated, may hold values from 0.1 to 1.9
- norm_bias: float32 [320], replicated, may hold values from -3 to 3
- conv_mid: bfloat16 [9, 320, 320], replicated, may hold values from -0.109375 to 0.109375
- conv_out: bfloat16 [16, 320], replicated, may hold values from -0.3125 to 0.3125
Outputs:
- iterate: float32 [8, 16, 64, 128], P('tm', None, 'strip')
- residual: float32 [8, 16, 64, 128], P('tm', None, 'strip')
The draws below stay inside these ranges and needn't reach their ends.
Inputs may be any that keep to these rules, and one draw needn't show every extreme that they name: mix_table[j, i] is 0 for i > j and lies in 64 to 128 for i = j.
All inputs are finite; a program needn't handle non-finite values.
Results may differ from the reference program's by a relative error of at most 0.001.
Values may be sent and summed in bfloat16 or wider, within the bound.
No kernel may reach another device: no remote copies, remote signals or barrier semaphores. Data moves between devices by JAX's collectives and lax.ppermute only.
A program may use at most 128 MiB of HBM per device.

```python
import math
import jax
import jax.numpy as jnp
from jax import lax

CIN = 16
CH = 320
GROUPS = 32
NTIME = 1000
HIST = 3
ITERS = 2
WIDTH = 128
STEPS = 8
HEIGHT = 64


def draw_start_state(key, part):
    shape = (CIN, HEIGHT, WIDTH)
    rows = jnp.arange(HEIGHT, dtype=jnp.float32) / max(HEIGHT - 1, 1)
    base = jnp.clip(jax.random.normal(key, shape, jnp.float32), -6.0, 6.0)
    return base * (3.0 ** rows)[:, None]


def draw_trajectory(key, part):
    shape = (STEPS, CIN, HEIGHT, WIDTH)
    rows = jnp.arange(HEIGHT, dtype=jnp.float32) / max(HEIGHT - 1, 1)
    base = jnp.clip(jax.random.normal(key, shape, jnp.float32), -4.0, 4.0)
    return base * (3.0 ** rows)[:, None] + (1.0 + 3.0 * rows)[:, None]


def draw_mix_table(key, part):
    first_key, second_key = jax.random.split(jax.random.fold_in(key, 11))
    below = jax.random.randint(first_key, (STEPS, STEPS), -64, 65, dtype=jnp.int32)
    middle = jax.random.randint(second_key, (STEPS,), 64, 129, dtype=jnp.int32)
    row_index = jnp.arange(STEPS, dtype=jnp.int32)[:, None]
    col_index = jnp.arange(STEPS, dtype=jnp.int32)[None, :]
    middle_full = jnp.broadcast_to(middle[:, None], (STEPS, STEPS))
    return jnp.where(col_index < row_index, below, jnp.where(col_index == row_index, middle_full, jnp.zeros_like(below)))


def plant(drawn, own_key, low, high):
    longest = drawn.shape.index(max(drawn.shape))
    spots = []
    for shift in (0, 1):
        where = [jax.random.randint(jax.random.fold_in(own_key, axis), (), 0, length) for axis, length in enumerate(drawn.shape)]
        where[longest] = (where[longest] + shift) % drawn.shape[longest]
        spots.append(tuple(where))
    return drawn.at[spots[0]].set(low).at[spots[1]].set(high)


def steps_of(stream_key, dims, pieces, smallest, high):
    level, own = 1.0, jax.random.fold_in(stream_key, 6)
    for dim, shards_of in pieces:
        steps = jnp.exp(jax.random.uniform(jax.random.fold_in(own, dim), (shards_of,), jnp.float32, smallest / len(pieces), high / len(pieces)))
        level = level * jnp.repeat(steps, dims[dim] // shards_of).reshape([-1 if axis == dim else 1 for axis in range(len(dims))])
    return level


def gaussian(own_key, shape, deviation, bound, cuts=(), kind=jnp.bfloat16):
    level = steps_of(own_key, shape, cuts, -0.22, 0.18) if cuts else 1.0
    drawn = jax.random.normal(own_key, shape, jnp.float32) * deviation * level
    return jnp.minimum(jnp.maximum(drawn, -bound), bound).astype(kind)


def setup_inputs(seed: int = 0) -> dict:
    key_list = jax.random.split(jax.random.key(seed), 14)
    return {
        "start_state": draw_start_state(jax.random.fold_in(key_list[13], 71), 0),
        "trajectory": draw_trajectory(jax.random.fold_in(key_list[13], 71), 0),
        "history": gaussian(key_list[2], (HIST, STEPS, CIN, HEIGHT, WIDTH), 1.0, 6.0, ((1, 4), (3, 8)), jnp.float32),
        "history_length": plant(jax.random.randint(key_list[3], (STEPS,), 1, HIST + 1), jax.random.fold_in(key_list[3], 1), 1, HIST).astype(jnp.int32),
        "timesteps": plant(jax.random.randint(key_list[4], (STEPS,), 0, NTIME), jax.random.fold_in(key_list[4], 1), 0, NTIME - 1).astype(jnp.int32),
        "step_size": jnp.clip(jnp.exp(math.log(0.2) - 1.3862944 * jax.random.uniform(key_list[5], (STEPS,), jnp.float32) ** steps_of(key_list[5], (STEPS,), ((0, 4),), -0.2, 0.2)), 0.05, 0.2),
        "mix_table": draw_mix_table(jax.random.fold_in(key_list[13], 71), 0),
        "time_table": gaussian(key_list[7], (NTIME, CH), 1.0, 6.0, (), jnp.float32),
        "conv_in": gaussian(key_list[8], (9, CH, CIN), (9 * CIN) ** -0.5, 0.5),
        "norm_gain": jnp.clip(1.0 + 0.18 * jax.random.normal(key_list[9], (CH,), jnp.float32), 0.1, 1.9),
        "norm_bias": gaussian(key_list[10], (CH,), 0.5, 3.0, (), jnp.float32),
        "conv_mid": gaussian(key_list[11], (9, CH, CH), (9 * CH) ** -0.5, 0.109375),
        "conv_out": gaussian(key_list[12], (CIN, CH), CH ** -0.5, 0.3125),
    }


epsilon = 1e-05
coefficient_unit = 256.0

def convolve(padded_rows, weights):
    height = padded_rows.shape[-2] - 2
    width = padded_rows.shape[-1]
    padded = jnp.pad(padded_rows, ((0, 0), (0, 0), (1, 1))).astype(jnp.float32)
    total = jnp.zeros((weights.shape[1], height, width), jnp.float32)
    for row_tap in range(3):
        for col_tap in range(3):
            window = padded[:, row_tap:row_tap + height, col_tap:col_tap + width]
            total = total + jnp.einsum('oc,chw->ohw', weights[3 * row_tap + col_tap].astype(jnp.float32), window, precision=lax.Precision.HIGHEST)
    return total

def denoise(state_bf, embed_row, conv_in, norm_gain, norm_bias, conv_mid, conv_out):
    early = convolve(jnp.pad(state_bf, ((0, 0), (1, 1), (0, 0))), conv_in) + embed_row[:, None, None]
    channels, height, width = early.shape
    grouped = early.reshape(GROUPS, channels // GROUPS, height, width)
    mean = lax.optimization_barrier(jnp.mean(grouped, axis=(1, 2, 3), keepdims=True))
    variance = lax.optimization_barrier(jnp.mean((grouped - mean) * (grouped - mean), axis=(1, 2, 3), keepdims=True))
    normed = ((grouped - mean) / jnp.sqrt(variance + epsilon)).reshape(channels, height, width)
    hidden = jax.nn.silu(normed * norm_gain[:, None, None] + norm_bias[:, None, None]).astype(jnp.bfloat16)
    late = convolve(jnp.pad(hidden, ((0, 0), (1, 1), (0, 0))), conv_mid)
    active = jax.nn.silu(late).astype(jnp.bfloat16)
    return jnp.einsum('oc,chw->ohw', conv_out.astype(jnp.float32), active.astype(jnp.float32), precision=lax.Precision.HIGHEST)

def reference(start_state, trajectory, history, history_length, timesteps, step_size, mix_table, time_table, conv_in, norm_gain, norm_bias, conv_mid, conv_out):
    selector = (timesteps[:, None] == jnp.arange(time_table.shape[0], dtype=jnp.int32)[None, :]).astype(jnp.float32)
    embedding = jnp.dot(selector, time_table, precision=lax.Precision.HIGHEST)
    coefficient = mix_table.astype(jnp.float32) / coefficient_unit
    levels = jnp.arange(history.shape[0], dtype=jnp.int32)[:, None]
    live = (levels < history_length[None, :]).astype(jnp.float32) / history_length[None, :].astype(jnp.float32)
    state = trajectory
    past = history
    residual = jnp.zeros_like(trajectory)
    for sweep in range(ITERS):
        field = lax.map(lambda pair: denoise(pair[0], pair[1], conv_in, norm_gain, norm_bias, conv_mid, conv_out), (state.astype(jnp.bfloat16), embedding))
        drift = step_size[:, None, None, None] * field
        running = jnp.cumsum(drift, axis=0)
        before = jnp.concatenate([jnp.zeros_like(drift[:1]), running[:-1]], axis=0)
        guess = start_state[None] + before
        residual = guess - state
        anchor = residual - jnp.einsum('ms,mschw->schw', live, past, precision=lax.Precision.HIGHEST)
        correction = jnp.einsum('ji,ichw->jchw', coefficient, anchor, precision=lax.Precision.HIGHEST)
        state = guess + correction
        past = jnp.concatenate([residual[None], past[:-1]], axis=0)
    return (state, residual)
```

```python
import functools

import jax
import jax.numpy as jnp
from jax import lax
from jax.experimental import pallas as pl
from jax.experimental.pallas import tpu as pltpu
from jax.sharding import PartitionSpec as P

GROUPS = 32
ITERS = 2
TAPS = 3
EDGE = 2
LANES = 128
PIECES = 3

epsilon = 1e-05
coefficient_unit = 256.0

f32 = jnp.float32
bf16 = jnp.bfloat16
HIGHEST = lax.Precision.HIGHEST


def lane_shifts(x):
    lane = lax.broadcasted_iota(jnp.int32, x.shape, 1)
    zero = jnp.zeros_like(x)
    left = jnp.where(lane == 0, zero, pltpu.roll(x, 1, 1))
    right = jnp.where(lane == LANES - 1, zero, pltpu.roll(x, LANES - 1, 1))
    return left.astype(bf16), x.astype(bf16), right.astype(bf16)


def split3(x):
    hi = x.astype(bf16).astype(f32)
    mid = (x - hi).astype(bf16).astype(f32)
    low = (x - hi - mid).astype(bf16).astype(f32)
    return hi, mid, low


def row_sum(x):
    return jnp.sum(x, axis=1, keepdims=True)


def indicator(groups, channels):
    group = lax.broadcasted_iota(jnp.int32, (groups, channels), 0)
    channel = lax.broadcasted_iota(jnp.int32, (groups, channels), 1)
    return (channel // (channels // groups) == group).astype(f32)


def group_sums(columns):
    channels = columns[0].shape[0]
    lane = lax.broadcasted_iota(jnp.int32, (channels, LANES), 1)
    stack = jnp.zeros((channels, LANES), f32)
    for k, column in enumerate(columns):
        here = (lane % len(columns)) == k
        stack = jnp.where(here, column, stack)
    return jnp.dot(indicator(GROUPS, channels), stack, precision=HIGHEST, preferred_element_type=f32)


def ones_rows(step, steps, cells, rows):
    row = lax.broadcasted_iota(jnp.int32, (rows, cells), 0)
    return ((row >= PIECES * step) & (row < PIECES * (step + 1))).astype(bf16)


class Sizes:
    def __init__(self, mesh, trajectory, history, conv_mid):
        self.steps, self.cin, self.rows, self.width = trajectory.shape
        self.hist = history.shape[0]
        self.channels = conv_mid.shape[1]
        self.groups_tm = mesh.shape["tm"]
        self.strips = mesh.shape["strip"]
        self.total = self.steps * self.groups_tm
        self.plane = self.cin * self.rows
        self.edges = self.steps * 2 * EDGE * self.cin
        self.message = self.edges + GROUPS
        self.taps = TAPS * TAPS * self.cin
        self.extra = 16
        self.depth = self.taps + self.extra
        self.count = float(self.channels // GROUPS * self.rows * self.strips * self.width)
        assert self.width == LANES and PIECES * self.steps <= self.extra


def strip_message(z, state_ref, win_ref, msg_ref, xmat_ref, patch):
    columns = []
    inner = z.rows - 2
    cells = inner * LANES
    for s in range(z.steps):
        for r in range(z.rows):
            x = state_ref[pl.ds(s * z.plane + r, z.cin, stride=z.rows), :].astype(bf16)
            xmat_ref[s * z.cin : (s + 1) * z.cin, r * LANES : (r + 1) * LANES] = x
            for b, y in enumerate(lane_shifts(x.astype(f32))):
                for a in range(TAPS):
                    out = r - a
                    if 0 <= out < inner:
                        top = (a * TAPS + b) * z.cin
                        patch[top : top + z.cin, out * LANES : (out + 1) * LANES] = y
            edge = r if r < EDGE else r - z.rows + 2 * EDGE
            if r < EDGE or r >= z.rows - EDGE:
                top = (s * 2 * EDGE + edge) * z.cin
                for k in range(z.strips):
                    msg_ref[k, top : top + z.cin, :] = x
        patch[z.taps :, :] = ones_rows(s, z.steps, cells, z.extra)
        early = jnp.dot(win_ref[...], patch[...], preferred_element_type=f32)
        total = square = None
        for k in range(inner):
            e = early[:, k * LANES : (k + 1) * LANES]
            total = e if total is None else total + e
            square = e * e if square is None else square + e * e
        columns += [row_sum(total), row_sum(square)]
    sums = group_sums(columns)
    hi, mid, low = split3(sums)
    lane = lax.broadcasted_iota(jnp.int32, sums.shape, 1)
    n = len(columns)
    packed = jnp.where(lane < n, hi, jnp.where(lane < 2 * n, mid, jnp.where(lane < 3 * n, low, 0.0))).astype(bf16)
    for k in range(z.strips):
        msg_ref[k, z.edges :, :] = packed


def first_kernel(z, state_ref, win_ref, msg_ref, xmat_ref, patch):
    strip_message(z, state_ref, win_ref, msg_ref, xmat_ref, patch)


def steps_kernel(z, mix_ref, square_ref, live_ref, state_ref, hist_ref, out_ref):
    here = lax.axis_index("tm")
    n = z.plane
    loads, carried, keep = [], [], []
    for s in range(z.steps):
        state = state_ref[s * n : (s + 1) * n, :]
        h = jnp.zeros_like(state)
        k = jnp.zeros_like(state)
        for m in range(z.hist):
            piece = hist_ref[(m * z.steps + s) * n : (m * z.steps + s + 1) * n, :]
            h = h + live_ref[m, s] * piece
            if m + 1 < z.hist:
                k = k + live_ref[m + 1, s] * piece
        loads.append(state + h)
        carried.append(live_ref[0, s] * state - k)
    for g in range(z.groups_tm):
        for s in range(z.steps):
            j = g * z.steps + s
            first = second = None
            for q in range(z.steps):
                i = here * z.steps + q
                c = mix_ref[j, i]
                one = c * loads[q]
                two = square_ref[j, i] * loads[q] + c * carried[q]
                first = one if first is None else first + one
                second = two if second is None else second + two
            out_ref[g, s * n : (s + 1) * n, :] = first
            out_ref[g, (z.steps + s) * n : (z.steps + s + 1) * n, :] = second
        tail = [jnp.full((1, LANES), live_ref[0, s], f32) for s in range(z.steps)]
        tail.append(jnp.zeros((8 - z.steps, LANES), f32))
        out_ref[g, 2 * z.steps * n :, :] = jnp.concatenate(tail, axis=0)


def denoise_kernel(z, msg_ref, xmat_ref, win_ref, wmid_ref, wout_ref, gain_ref, step_ref, drift_ref, edge_patch, own_patch, hidden, drift):
    me = lax.axis_index("strip")
    strips = z.strips
    outer = z.rows + 2
    stat = jnp.zeros((GROUPS, LANES), f32)
    for k in range(strips):
        stat = stat + msg_ref[k, z.edges :, :].astype(f32)
    columns = []
    earlies = []
    above = jnp.maximum(me - 1, 0)
    below = jnp.minimum(me + 1, strips - 1)
    has_above = (me > 0).astype(f32)
    has_below = (me < strips - 1).astype(f32)

    def tile(k, s, e):
        top = (s * 2 * EDGE + e) * z.cin
        return msg_ref[k, top : top + z.cin, :].astype(f32)

    for s in range(z.steps):
        zero = jnp.zeros((z.cin, LANES), bf16)
        for k in range(strips):
            for e in range(2 * EDGE):
                for b, y in enumerate(lane_shifts(tile(k, s, e))):
                    places = []
                    if e == 0:
                        places = [(2 * k, 1)] + ([(2 * k - 1, 2)] if k > 0 else [])
                    elif e == 1:
                        places = [(2 * k, 2)]
                    elif e == 2:
                        places = [(2 * k + 1, 0)]
                    else:
                        places = [(2 * k + 1, 1)] + ([(2 * k + 2, 0)] if k + 1 < strips else [])
                    for cell, a in places:
                        top = (a * TAPS + b) * z.cin
                        edge_patch[top : top + z.cin, cell * LANES : (cell + 1) * LANES] = y
        for b in range(TAPS):
            top = b * z.cin
            edge_patch[top : top + z.cin, 0:LANES] = zero
            top = (2 * TAPS + b) * z.cin
            edge_patch[top : top + z.cin, (2 * strips - 1) * LANES :] = zero
        edge_patch[z.taps :, :] = ones_rows(s, z.steps, 2 * strips * LANES, z.extra)
        early = jnp.dot(win_ref[...], edge_patch[...], preferred_element_type=f32)
        total = square = None
        for k in range(2 * strips):
            e = early[:, k * LANES : (k + 1) * LANES]
            total = e if total is None else total + e
            square = e * e if square is None else square + e * e
        columns += [row_sum(total), row_sum(square)]
        for r in range(-EDGE, z.rows + EDGE):
            if r < 0:
                x = tile(above, s, 2 * EDGE + r) * has_above
            elif r >= z.rows:
                x = tile(below, s, r - z.rows) * has_below
            else:
                x = xmat_ref[s * z.cin : (s + 1) * z.cin, r * LANES : (r + 1) * LANES].astype(f32)
            for b, y in enumerate(lane_shifts(x)):
                for a in range(TAPS):
                    out = r + EDGE - a
                    if 0 <= out < outer:
                        top = (a * TAPS + b) * z.cin
                        own_patch[s, top : top + z.cin, out * LANES : (out + 1) * LANES] = y
        own_patch[s, z.taps :, :] = ones_rows(s, z.steps, outer * LANES, z.extra)

    n = len(columns)
    stat = stat + pltpu.roll(stat, LANES - n, 1) + pltpu.roll(stat, LANES - 2 * n, 1)
    stat = stat + group_sums(columns)
    lane = lax.broadcasted_iota(jnp.int32, (GROUPS, LANES), 1)
    spread = jnp.zeros((GROUPS, LANES), f32)
    for s in range(z.steps):
        mean = stat[:, 2 * s : 2 * s + 1] / z.count
        variance = stat[:, 2 * s + 1 : 2 * s + 2] / z.count - mean * mean
        inverse = 1.0 / jnp.sqrt(jnp.maximum(variance, 0.0) + epsilon)
        spread = jnp.where(lane == 2 * s, mean, jnp.where(lane == 2 * s + 1, inverse, spread))
    channel = lax.broadcasted_iota(jnp.int32, (z.channels, GROUPS), 0)
    group = lax.broadcasted_iota(jnp.int32, (z.channels, GROUPS), 1)
    expand = (channel // (z.channels // GROUPS) == group).astype(f32)
    spread = jnp.dot(expand, spread, precision=HIGHEST, preferred_element_type=f32)
    gain, bias = gain_ref[:, 0:1], gain_ref[:, 1:2]
    for s in range(z.steps):
        scale = gain * spread[:, 2 * s + 1 : 2 * s + 2]
        shift = bias - spread[:, 2 * s : 2 * s + 1] * scale
        early = jnp.dot(win_ref[...], own_patch[s], preferred_element_type=f32)
        for r in range(outer):
            v = early[:, r * LANES : (r + 1) * LANES] * scale + shift
            v = v / (1.0 + jnp.exp(-v))
            if r == 0:
                v = v * has_above
            elif r == outer - 1:
                v = v * has_below
            v = v.astype(bf16).astype(f32)
            for b, y in enumerate(lane_shifts(v)):
                hidden[b * z.channels : (b + 1) * z.channels, r * LANES : (r + 1) * LANES] = y
        late = None
        for a in range(TAPS):
            part = jnp.dot(wmid_ref[a], hidden[:, a * LANES : (a + z.rows) * LANES], preferred_element_type=f32)
            late = part if late is None else late + part
        active = (late / (1.0 + jnp.exp(-late))).astype(bf16)
        field = jnp.dot(wout_ref[...], active, preferred_element_type=f32) * step_ref[s]
        for r in range(z.rows):
            drift[pl.ds(s * z.plane + r, z.cin, stride=z.rows), :] = field[:, r * LANES : (r + 1) * LANES]
    drift_ref[...] = drift[...].astype(bf16)


def guesses(z, drift_ref, start_ref):
    running = start_ref[...]
    out = []
    for i in range(z.total):
        out.append(running)
        if i + 1 < z.total:
            g, s = divmod(i, z.steps)
            running = running + drift_ref[g, s * z.plane : (s + 1) * z.plane, :].astype(f32)
    return out


def next_kernel(z, mix_ref, drift_ref, start_ref, given_ref, win_ref, state_ref, msg_ref, xmat_ref, patch):
    here = lax.axis_index("tm")
    n = z.plane
    for s in range(z.steps):
        j = here * z.steps + s
        state = None
        for i, g in enumerate(guesses(z, drift_ref, start_ref)):
            weight = mix_ref[j, i] + (i == j).astype(f32)
            state = weight * g if state is None else state + weight * g
        for g in range(z.groups_tm):
            state = state - given_ref[g, s * n : (s + 1) * n, :]
        state_ref[s * n : (s + 1) * n, :] = state
    strip_message(z, state_ref, win_ref, msg_ref, xmat_ref, patch)


def base_kernel(z, mix_ref, square_ref, drift_ref, start_ref, given_ref, base_ref):
    here = lax.axis_index("tm")
    n = z.plane
    for s in range(z.steps):
        j = here * z.steps + s
        base = None
        for g in range(z.groups_tm):
            piece = given_ref[g, (z.steps + s) * n : (z.steps + s + 1) * n, :]
            base = piece if base is None else base + piece
        for i, guess in enumerate(guesses(z, drift_ref, start_ref)):
            g, q = divmod(i, z.steps)
            live = given_ref[g, 2 * z.steps * n + q : 2 * z.steps * n + q + 1, :]
            weight = mix_ref[j, i] * (1.0 + live) + square_ref[j, i]
            base = base - weight * guess
        base_ref[s * n : (s + 1) * n, :] = base


def last_kernel(z, mix_ref, drift_ref, start_ref, state_ref, base_ref, iterate_ref, residual_ref):
    here = lax.axis_index("tm")
    n = z.plane
    for s in range(z.steps):
        j = here * z.steps + s
        at = slice(s * n, (s + 1) * n)
        own = jnp.zeros((n, LANES), f32)
        mixed = base_ref[at, :]
        for i, g in enumerate(guesses(z, drift_ref, start_ref)):
            own = jnp.where(i == j, g, own)
            mixed = mixed + mix_ref[j, i] * g
        iterate_ref[at, :] = own + mixed
        residual_ref[at, :] = own - state_ref[at, :]


def call(body, outs, scratch, scalars, arrays):
    vmem = pl.BlockSpec(memory_space=pltpu.VMEM)
    smem = pl.BlockSpec(memory_space=pltpu.SMEM)
    return pl.pallas_call(
        body,
        out_shape=[jax.ShapeDtypeStruct(s, d) for s, d in outs],
        in_specs=[smem] * len(scalars) + [vmem] * len(arrays),
        out_specs=[vmem] * len(outs),
        scratch_shapes=scratch,
        compiler_params=pltpu.CompilerParams(vmem_limit_bytes=60 << 20),
    )(*scalars, *arrays)


def shards(
    mesh,
    start_state,
    trajectory,
    history,
    history_length,
    timesteps,
    step_size,
    mix_table,
    time_table,
    conv_in,
    norm_gain,
    norm_bias,
    conv_mid,
    conv_out,
):
    z = Sizes(mesh, trajectory, history, conv_mid)
    here = functools.partial
    selector = (jnp.arange(time_table.shape[0], dtype=jnp.int32)[:, None] == timesteps[None, :]).astype(f32)
    embedding = lax.dot_general(time_table, selector, (((0,), (0,)), ((), ())), precision=HIGHEST)
    hi = lax.reduce_precision(embedding, 8, 7)
    mid = lax.reduce_precision(embedding - hi, 8, 7)
    low = lax.reduce_precision(embedding - hi - mid, 8, 7)
    pieces = jnp.stack([hi, mid, low], axis=2).reshape(z.channels, PIECES * z.steps).astype(bf16)
    pieces = jnp.pad(pieces, ((0, 0), (0, z.extra - PIECES * z.steps)))
    win = jnp.concatenate([conv_in.transpose(1, 0, 2).reshape(z.channels, z.taps), pieces], axis=1)
    wmid = conv_mid.reshape(TAPS, TAPS, z.channels, z.channels).transpose(0, 2, 1, 3)
    wmid = wmid.reshape(TAPS, z.channels, TAPS * z.channels)
    gain = jnp.stack([norm_gain, norm_bias], axis=1)
    mix = mix_table.astype(f32) / coefficient_unit
    square = jnp.dot(mix, mix, precision=HIGHEST)
    levels = jnp.arange(z.hist, dtype=jnp.int32)[:, None]
    live = (levels < history_length[None, :]).astype(f32) / history_length[None, :].astype(f32)
    flat = z.steps * z.plane
    state = trajectory.reshape(flat, LANES)
    start = start_state.reshape(z.plane, LANES)

    message = [((z.strips, z.message, LANES), bf16), ((z.steps * z.cin, z.rows * LANES), bf16)]
    inner_patch = [pltpu.VMEM((z.depth, (z.rows - 2) * LANES), bf16)]
    msg, xmat = call(here(first_kernel, z), message, inner_patch, [], [state, win])
    share = call(
        here(steps_kernel, z),
        [((z.groups_tm, 2 * flat + 8, LANES), f32)],
        [],
        [mix, square, live],
        [state, history.reshape(z.hist * flat, LANES)],
    )[0]
    given = lax.all_to_all(share, "tm", 0, 0, tiled=True)

    def denoise(msg, xmat):
        outer = z.rows + 2
        got = lax.all_to_all(msg, "strip", 0, 0, tiled=True)
        drift = call_denoise(got, xmat)
        return lax.all_gather(drift, "tm")

    def call_denoise(got, xmat):
        outer = z.rows + 2
        smem = pl.BlockSpec(memory_space=pltpu.SMEM)
        vmem = pl.BlockSpec(memory_space=pltpu.VMEM)
        return pl.pallas_call(
            here(denoise_kernel, z),
            out_shape=jax.ShapeDtypeStruct((flat, LANES), bf16),
            in_specs=[vmem] * 6 + [smem],
            out_specs=vmem,
            scratch_shapes=[
                pltpu.VMEM((z.depth, 2 * z.strips * LANES), bf16),
                pltpu.VMEM((z.steps, z.depth, outer * LANES), bf16),
                pltpu.VMEM((TAPS * z.channels, outer * LANES), bf16),
                pltpu.VMEM((flat, LANES), f32),
            ],
            compiler_params=pltpu.CompilerParams(vmem_limit_bytes=60 << 20),
        )(got, xmat, win, wmid, conv_out, gain, step_size)

    drift = denoise(msg, xmat)
    state, msg, xmat = call(
        here(next_kernel, z), [((flat, LANES), f32)] + message, inner_patch, [mix], [drift, start, given, win]
    )
    base = call(here(base_kernel, z), [((flat, LANES), f32)], [], [mix, square], [drift, start, given])[0]
    drift = denoise(msg, xmat)
    iterate, residual = call(
        here(last_kernel, z), [((flat, LANES), f32)] * 2, [], [mix], [drift, start, state, base]
    )
    return iterate.reshape(trajectory.shape), residual.reshape(trajectory.shape)


def solution(mesh):
    return jax.shard_map(
        functools.partial(shards, mesh),
        mesh=mesh,
        in_specs=(
            P(None, "strip", None),
            P("tm", None, "strip", None),
            P(None, "tm", None, "strip", None),
            P("tm"),
            P("tm"),
            P("tm"),
            P(),
            P(),
            P(),
            P(),
            P(),
            P(),
            P(),
        ),
        out_specs=(P("tm", None, "strip", None), P("tm", None, "strip", None)),
        check_vma=False,
    )
```
